32 devices in a mesh: lon: 8 (over z, y), lat: 4 (over x, core).
Axes of the slice: x: 2, y: 2, z: 4, core: 2. Of those that a mesh axis runs over, the one named last changes fastest.
Arguments:
- layer_depth: float32 [32, 256, 1024], P(None, 'lat', 'lon'), may hold values from 0.5 to 1.5
- momentum: float32 [2, 32, 256, 1024], P(None, None, 'lat', 'lon'), may hold values from -1 to 1
- gravity: float32 [32], replicated, may hold values from 1 to 4
- absorption: float32 [56, 32], replicated, may hold values from 0.003 to 0.06
- solar_flux: float32 [56], replicated, may hold values from 0.125 to 1.25
- cos_zenith: float32 [256, 1024], P('lat', 'lon'), may hold values from 0.05 to 1
- sunlit: int32 [256, 8], P('lat', 'lon'), may hold values from 0 to 1
- owner_index: int32 [256, 8], P('lat', 'lon'), may hold values from 0 to 7, as said below
- slot_index: int32 [256, 8], P('lat', 'lon'), may hold values from 0 to 7, as said below
- received_counts: int32 [4, 8, 8], P('lat', 'lon'), may hold values from 0 to 8, as said below
Outputs:
- depth_out: float32 [32, 256, 1024], P(None, 'lat', 'lon')
- momentum_out: float32 [2, 32, 256, 1024], P(None, None, 'lat', 'lon')
- heating: float32 [32, 256, 1024], P(None, 'lat', 'lon')
- ledger: float32 [4, 8, 32], P('lat', 'lon')
The draws below stay inside these ranges and needn't reach their ends.
Inputs may be any that keep to these rules, and one draw needn't show every extreme that they name: For dark blocks owner_index is the block's own lon index and slot_index is 0; sunlit blocks of one device go to distinct (owner, slot) pairs. `slot_index`: the slots of the blocks that one device hands to one owner are 0, 1, ... without gaps. received_counts agrees with sunlit and owner_index; each owner receives at most 32 blocks in all from its lat index.
All inputs are finite; a program needn't handle non-finite values.
Results may differ from the reference program's by a relative error of at most 0.00014.
Values sent between devices are 32-bit elements; how exact they have to be, the bound alone decides.
No kernel may reach another device: no remote copies, remote signals or barrier semaphores. Data moves between devices by JAX's collectives and lax.ppermute only.
A program may use at most 128 MiB of HBM per device.

```python
import math
import jax
import jax.numpy as jnp
from jax import lax

LAYERS = 32
BANDS = 56
BLOCK = 128
CLAT = 64
STEPS = 2
ROWS = 256
COLS = 1024
CAP = 8
LOAD = 32
N_LON = 8
N_LAT = 4


def balancing_plan(key):
    plan_key = jax.random.fold_in(key, 7)
    key_arc, key_count, key_order = jax.random.split(plan_key, 3)
    arc_start = jax.random.randint(key_arc, (), 0, N_LON)
    lon_ids = jnp.arange(N_LON).astype(jnp.int32)
    distance = (lon_ids - arc_start) % N_LON
    day_side = distance < N_LON // 2
    evening = distance == N_LON // 2 - 1
    least_lit = (CLAT // N_LON - 1) * N_LON + 1
    lit_count = jax.random.randint(key_count, (N_LAT,), least_lit, CLAT + 1)
    order_keys = jax.random.split(key_order, N_LAT)
    row_order = jax.vmap(lambda each_key: jax.random.permutation(each_key, CLAT))(order_keys)
    evening_lit = (row_order < lit_count[:, None]).reshape(ROWS)
    lit_blocks = jnp.where(evening[None, :], evening_lit[:, None], day_side[None, :]).astype(jnp.int32)
    grouped = lit_blocks.reshape(N_LAT, CLAT, N_LON)
    rank = (jnp.cumsum(grouped, axis=1) - grouped).reshape(ROWS, N_LON)
    owners = jnp.where(lit_blocks == 1, (lon_ids[None, :] + rank) % N_LON, lon_ids[None, :]).astype(jnp.int32)
    slots = jnp.where(lit_blocks == 1, rank // N_LON, 0).astype(jnp.int32)
    owner_hot = (owners.reshape(N_LAT, CLAT, 1, N_LON) == lon_ids[None, None, :, None]).astype(jnp.int32)
    block_counts = jnp.sum(owner_hot * grouped[:, :, None, :], axis=1).astype(jnp.int32)
    return (lit_blocks, owners, slots, block_counts)


def draw_sunlit(key, part):
    return balancing_plan(key)[0]


def draw_owner_index(key, part):
    return balancing_plan(key)[1]


def draw_slot_index(key, part):
    return balancing_plan(key)[2]


def draw_received_counts(key, part):
    return balancing_plan(key)[3]


def level_of(stream_key, extent, shards, least, largest):
    factor_of = 1.0
    for dim, shards_of in shards:
        steps = jax.random.uniform(jax.random.fold_in(jax.random.fold_in(stream_key, 6), dim), (shards_of,), jnp.float32, least / len(shards), largest / len(shards))
        factor_of = factor_of * jnp.repeat(jnp.exp(steps), extent[dim] // shards_of).reshape((-1,) + (1,) * (len(extent) - 1 - dim))
    return factor_of


def scatter_about(key, shape, width, bound, cuts=(), kind=jnp.bfloat16):
    values = width * jax.random.normal(key, shape, jnp.float32)
    if cuts:
        values = values * level_of(key, shape, cuts, -0.22, 0.18)
    return jnp.clip(values, -bound, bound).astype(kind)


def setup_inputs(seed: int = 0) -> dict:
    key_list = jax.random.split(jax.random.key(seed), 11)
    return {
        "layer_depth": jnp.clip(0.5 + 1.0 * jax.random.uniform(key_list[0], (LAYERS, ROWS, COLS), jnp.float32) ** level_of(key_list[0], (LAYERS, ROWS, COLS), ((1, 4), (2, 8)), -0.2, 0.2), 0.5, 1.5),
        "momentum": scatter_about(key_list[1], (2, LAYERS, ROWS, COLS), 0.3, 1.0, ((2, 4), (3, 8)), jnp.float32),
        "gravity": jnp.clip(jnp.exp(jax.random.uniform(key_list[2], (LAYERS,), jnp.float32, math.log(1.0), math.log(4.0))), 1.0, 4.0),
        "absorption": jnp.clip(jnp.exp(jax.random.uniform(key_list[3], (BANDS, LAYERS), jnp.float32, math.log(0.003), math.log(0.06))), 0.003, 0.06),
        "solar_flux": jnp.clip(jnp.exp(jax.random.uniform(key_list[4], (BANDS,), jnp.float32, math.log(0.125), math.log(1.25))), 0.125, 1.25),
        "cos_zenith": jnp.clip(0.05 + 0.95 * jax.random.uniform(key_list[5], (ROWS, COLS), jnp.float32) ** level_of(key_list[5], (ROWS, COLS), ((0, 4), (1, 8)), -0.2, 0.2), 0.05, 1.0),
        "sunlit": draw_sunlit(jax.random.fold_in(key_list[10], 71), 0),
        "owner_index": draw_owner_index(jax.random.fold_in(key_list[10], 71), 0),
        "slot_index": draw_slot_index(jax.random.fold_in(key_list[10], 71), 0),
        "received_counts": draw_received_counts(jax.random.fold_in(key_list[10], 71), 0),
    }


COURANT = 0.06
CORIOLIS = 0.08
LAT_START = 0.35
LAT_SPAN = 0.62

def physical_flux(state, velocity, gravity, along_axis):
    column_depth = state[0]
    normal = state[along_axis]
    other_mom = state[3 - along_axis]
    push_flux = normal * velocity + 0.5 * gravity * column_depth * column_depth
    carry_flux = other_mom * velocity
    if along_axis == 1:
        return jnp.stack([normal, push_flux, carry_flux])
    return jnp.stack([normal, carry_flux, push_flux])

def hll_flux(left_state, right_state, gravity, along_axis):
    velocity_left = left_state[along_axis] / left_state[0]
    velocity_right = right_state[along_axis] / right_state[0]
    wave_left = jnp.sqrt(gravity * left_state[0])
    wave_right = jnp.sqrt(gravity * right_state[0])
    lower_wave = jnp.minimum(jnp.minimum(velocity_left - wave_left, velocity_right - wave_right), 0.0)
    upper_wave = jnp.maximum(jnp.maximum(velocity_left + wave_left, velocity_right + wave_right), 0.0)
    flux_left = physical_flux(left_state, velocity_left, gravity, along_axis)
    flux_right = physical_flux(right_state, velocity_right, gravity, along_axis)
    return (upper_wave * flux_left - lower_wave * flux_right + lower_wave * upper_wave * (right_state - left_state)) / (upper_wave - lower_wave)

def advance(padded, gravity, latitude):
    centre = padded[:, :, 1:-1, 1:-1]
    east_flux = hll_flux(padded[:, :, 1:-1, :-1], padded[:, :, 1:-1, 1:], gravity, 1)
    north_flux = hll_flux(padded[:, :, :-1, 1:-1], padded[:, :, 1:, 1:-1], gravity, 2)
    cos_centre = jnp.cos(latitude[1:-1])[:, None]
    cos_face = jnp.cos(0.5 * (latitude[:-1] + latitude[1:]))[:, None]
    change = east_flux[..., 1:] - east_flux[..., :-1] + cos_face[1:] * north_flux[:, :, 1:] - cos_face[:-1] * north_flux[:, :, :-1]
    updated = centre - COURANT / cos_centre * change
    turning = CORIOLIS * jnp.sin(latitude[1:-1])[:, None]
    return jnp.stack([updated[0], updated[1] + turning * updated[2], updated[2] - turning * updated[1]])

def shortwave(column_depth, column_sun, absorption, solar_flux):
    layers = column_depth.shape[0]
    triangle = (jnp.arange(layers)[:, None] <= jnp.arange(layers)[None, :]).astype(jnp.float32)
    optical = absorption[:, :, None, None] * column_depth[None]
    optical_path = jnp.einsum('jk,bjnc->bknc', triangle, optical, precision=lax.Precision.HIGHEST)
    sun_cos = column_sun[None, None]
    down_flux = solar_flux[:, None, None, None] * sun_cos * jnp.exp(-optical_path / sun_cos)
    top_flux = solar_flux[:, None, None, None] * sun_cos
    flux_above = jnp.concatenate([top_flux, down_flux[:, :-1]], axis=1)
    absorbed = lax.optimization_barrier(jnp.sum(flux_above - down_flux, axis=0))
    return (absorbed / column_depth, absorbed)

def reference(layer_depth, momentum, gravity, absorption, solar_flux, cos_zenith, sunlit, owner_index, slot_index, received_counts):
    state = jnp.stack([layer_depth, momentum[0], momentum[1]])
    weight = gravity.reshape(-1, 1, 1)
    latitude = LAT_START + (jnp.arange(-1, ROWS + 1).astype(jnp.float32) + 0.5) * (LAT_SPAN / ROWS)
    for step_number in range(STEPS):
        padded = jnp.pad(state, ((0, 0), (0, 0), (1, 1), (0, 0)), mode='edge')
        padded = jnp.pad(padded, ((0, 0), (0, 0), (0, 0), (1, 1)), mode='wrap')
        state = advance(padded, weight, latitude)

    def per_row(row_number):
        column_depth = lax.dynamic_slice_in_dim(layer_depth, row_number, 1, 1)
        column_sun = lax.dynamic_slice_in_dim(cos_zenith, row_number, 1, 0)
        heating_part, absorbed = shortwave(column_depth, column_sun, absorption, solar_flux)
        lit_cols = jnp.repeat(sunlit[row_number].astype(jnp.float32), BLOCK)
        heating_part = heating_part[:, 0] * lit_cols[None, :]
        block_means = lax.optimization_barrier(jnp.mean(absorbed[:, 0].reshape(LAYERS, N_LON, BLOCK), axis=(0, 2)))
        return (heating_part, block_means)
    row_heating, block_means = lax.map(per_row, jnp.arange(ROWS).astype(jnp.int32))
    heating = jnp.transpose(row_heating, (1, 0, 2))
    lat_group = jnp.broadcast_to((jnp.arange(ROWS).astype(jnp.int32) // CLAT)[:, None], (ROWS, N_LON))
    source_lon = jnp.broadcast_to(jnp.arange(N_LON).astype(jnp.int32)[None, :], (ROWS, N_LON))
    ledger_table = jnp.zeros((N_LAT, N_LON, N_LON, CAP), jnp.float32)
    ledger_table = ledger_table.at[lat_group, source_lon, owner_index, slot_index].add(block_means * sunlit.astype(jnp.float32))
    count_ends = jnp.cumsum(received_counts, axis=-1).astype(jnp.int32)
    starts = count_ends - received_counts
    slot_order = jnp.arange(LOAD).astype(jnp.int32)
    source_of = jnp.minimum(lax.optimization_barrier(jnp.sum((count_ends[..., None, :] <= slot_order[:, None]).astype(jnp.int32), axis=-1)), N_LON - 1).astype(jnp.int32)
    slot_place = jnp.clip(slot_order - jnp.take_along_axis(starts, source_of, axis=-1), 0, CAP - 1).astype(jnp.int32)
    total_in = lax.optimization_barrier(jnp.sum(received_counts, axis=-1)).astype(jnp.int32)[..., None]
    group_idx = jnp.arange(N_LAT).astype(jnp.int32)[:, None, None]
    owner_idx = jnp.arange(N_LON).astype(jnp.int32)[None, :, None]
    picked = ledger_table[group_idx, source_of, owner_idx, slot_place]
    ledger = jnp.where(slot_order < total_in, picked, jnp.float32(0.0))
    return (state[0], state[1:], heating, ledger)
```

```python
import functools
import math

import jax
import jax.numpy as jnp
import numpy as np
from jax import lax
from jax.experimental import pallas as pl
from jax.experimental.pallas import tpu as pltpu
from jax.sharding import PartitionSpec as P

COURANT = 0.06
CORIOLIS = 0.08
LAT_START = 0.35
LAT_SPAN = 0.62
LANES = 128
SUB = 8
SUN_ROWS = 16
SUN_BANDS = 14
VMEM_LIMIT = 48 * 1024 * 1024


def params(**more):
    return pltpu.CompilerParams(vmem_limit_bytes=VMEM_LIMIT, **more)


def lane_index(rows=SUB):
    return lax.broadcasted_iota(jnp.int32, (rows, LANES), 1)


def latitude_table(lat_parts, band_rows):
    total = lat_parts * band_rows
    rows = np.arange(lat_parts)[:, None] * band_rows + np.arange(-2, LANES)[None, :]
    latitude = np.float32(LAT_START) + (rows.astype(np.float32) + np.float32(0.5)) * np.float32(LAT_SPAN / total)
    face = (np.float32(0.5) * (latitude[:, :-1] + latitude[:, 1:])).astype(np.float64)
    latitude = latitude.astype(np.float64)
    table = np.zeros((lat_parts, 8, LANES), np.float32)
    table[:, 0] = COURANT / np.cos(latitude[:, 1 : LANES + 1])
    table[:, 1] = np.cos(face[:, 1 : LANES + 1])
    table[:, 2] = np.cos(face[:, :LANES])
    table[:, 3] = CORIOLIS * np.sin(latitude[:, 1 : LANES + 1])
    return table.reshape(lat_parts * 8, LANES)


def cell(depth, east_mom, north_mom, gravity):
    inverse = 1.0 / depth
    east_vel = east_mom * inverse
    north_vel = north_mom * inverse
    weight = gravity * depth
    wave = weight * lax.rsqrt(weight)
    push = 0.5 * weight * depth
    cross = north_mom * east_vel
    return (
        depth,
        east_mom,
        north_mom,
        east_vel - wave,
        east_vel + wave,
        east_mom * east_vel + push,
        cross,
        north_vel - wave,
        north_vel + wave,
        north_mom * north_vel + push,
    )


def east_side(c):
    return (c[0], c[1], c[2], c[3], c[4], c[5], c[6])


def north_side(c):
    return (c[0], c[2], c[1], c[7], c[8], c[9], c[6])


def face(left, right):
    lower = jnp.minimum(jnp.minimum(left[3], right[3]), 0.0)
    upper = jnp.maximum(jnp.maximum(left[4], right[4]), 0.0)
    share = upper / (upper - lower)
    rise = right[1] - left[1]
    depth_flux = right[1] + share * (lower * (right[0] - left[0]) - rise)
    normal_flux = right[5] + share * (lower * rise - (right[5] - left[5]))
    other_flux = right[6] + share * (lower * (right[2] - left[2]) - (right[6] - left[6]))
    return depth_flux, normal_flux, other_flux


def turned(state, change, rate, turning):
    depth, east_mom, north_mom = (s - rate * c for s, c in zip(state, change))
    return depth, east_mom + turning * north_mom, north_mom - turning * east_mom


def roll(x, shift):
    return pltpu.roll(x, shift, 1)


def dynamics_kernel(
    band_rows,
    gravity_ref,
    table_ref,
    lanes_ref,
    depth_ref,
    mom_ref,
    north_ref,
    south_ref,
    west_ref,
    east_ref,
    own_west_ref,
    own_east_ref,
    depth_out,
    mom_out,
    middle,
):
    group = pl.program_id(0)
    lat = lax.axis_index("lat")
    at_first = lat == 0
    at_final = lat == lax.axis_size("lat") - 1
    lane = lane_index()
    sublane = lax.broadcasted_iota(jnp.int32, (SUB, LANES), 0)
    gravity = jnp.zeros((SUB, LANES), jnp.float32)
    for i in range(SUB):
        gravity = jnp.where(sublane == i, gravity_ref[group * SUB + i], gravity)

    both = jnp.concatenate([gravity, gravity], axis=0)
    lane2 = lane_index(2 * SUB)
    low_edge = (lane2 == 0) & at_first
    high_edge = (lane2 == band_rows + 1) & at_final

    def column(west, east):
        fields = []
        for f in range(3):
            x = jnp.concatenate([west(f), east(f)], axis=0)
            x = jnp.where(low_edge, roll(x, LANES - 1), x)
            fields.append(jnp.where(high_edge, roll(x, 1), x))
        return cell(*fields, both)

    columns = [
        column(lambda f: west_ref[f, 1], lambda f: own_east_ref[f, 1]),
        column(lambda f: west_ref[f, 0], lambda f: own_east_ref[f, 0]),
        column(lambda f: own_west_ref[f, 0], lambda f: east_ref[f, 0]),
        column(lambda f: own_west_ref[f, 1], lambda f: east_ref[f, 1]),
    ]
    rate_of, upper_cos, lower_cos, turn_of = (
        jnp.broadcast_to(lanes_ref[pl.ds(lat * 8 + q, 1), :], (2 * SUB, LANES)) for q in range(4)
    )
    fluxes = [face(east_side(a), east_side(b)) for a, b in zip(columns[:-1], columns[1:])]
    moved = []
    for k in (1, 2):
        c = columns[k]
        side = north_side(c)
        upper = face(side, tuple(roll(x, LANES - 1) for x in side))
        upper = (upper[0], upper[2], upper[1])
        change = tuple(
            fluxes[k][i] - fluxes[k - 1][i] + upper_cos * upper[i] - lower_cos * roll(upper[i], 1)
            for i in range(3)
        )
        moved.append(cell(*turned(c[:3], change, rate_of, turn_of), both))
    edge_fluxes = (fluxes[1], face(east_side(moved[0]), east_side(moved[1])))

    is_first_lane = lane == 0
    is_last_lane = lane == LANES - 1

    def advance_row(row, here, above, below_flux, edges):
        j = row + 1
        rate = table_ref[lat * 8, j]
        cos_upper = table_ref[lat * 8 + 1, j]
        turning = table_ref[lat * 8 + 3, j]
        upper = face(north_side(here), north_side(above))
        upper = (cos_upper * upper[0], cos_upper * upper[2], cos_upper * upper[1])
        side = east_side(here)
        flux = face(tuple(roll(x, 1) for x in side), side)
        change = []
        for i in range(3):
            west_edge = roll(edges[i][:SUB], lax.rem(2 * LANES - j, LANES))
            east_edge = roll(edges[i][SUB:], lax.rem(2 * LANES - 1 - j, LANES))
            west_flux = jnp.where(is_first_lane, west_edge, flux[i])
            east_flux = jnp.where(is_last_lane, east_edge, roll(flux[i], LANES - 1))
            change.append((east_flux - west_flux) + (upper[i] - below_flux[i]))
        return turned(here[:3], change, rate, turning), upper

    def weighted(row, below, here):
        cos_lower = table_ref[lat * 8 + 2, row + 1]
        flux = face(north_side(below), north_side(here))
        return cos_lower * flux[0], cos_lower * flux[2], cos_lower * flux[1]

    def block_row(row):
        window = pl.ds(row, SUB, stride=band_rows)
        return cell(depth_ref[window, :], mom_ref.at[0][window, :], mom_ref.at[1][window, :], gravity)

    def halo_row(ref, which, clamped, edge_row):
        window = pl.ds(edge_row, SUB, stride=band_rows)
        inside = (depth_ref[window, :], mom_ref.at[0][window, :], mom_ref.at[1][window, :])
        return cell(*(jnp.where(clamped, inside[f], ref[f, which]) for f in range(3)), gravity)

    def store_middle(row, state):
        for f in range(3):
            middle[f, pl.ds(pl.multiple_of((row + 1) * SUB, SUB), SUB), :] = state[f]

    def middle_row(row):
        window = pl.ds(pl.multiple_of((row + 1) * SUB, SUB), SUB)
        return cell(*(middle[f, window, :] for f in range(3)), gravity)

    edges = edge_fluxes[0]
    below, here = (halo_row(north_ref, which, at_first, 0) for which in (1, 0))
    flux = weighted(-1, below, here)
    above = block_row(0)
    state, flux = advance_row(-1, here, above, flux, edges)
    store_middle(-1, state)

    def first_step(unroll):
        def rows(n, carry):
            here, flux = carry
            for i in range(unroll):
                row = n * unroll + i
                above = block_row(row + 1)
                state, flux = advance_row(row, here, above, flux, edges)
                store_middle(row, state)
                here = above
            return here, flux

        return rows

    unroll = 7 if (band_rows - 1) % 7 == 0 else 1
    here, flux = lax.fori_loop(0, (band_rows - 1) // unroll, first_step(unroll), (above, flux))
    for row, above in (
        (band_rows - 1, halo_row(south_ref, 0, at_final, band_rows - 1)),
        (band_rows, halo_row(south_ref, 1, at_final, band_rows - 1)),
    ):
        state, flux = advance_row(row, here, above, flux, edges)
        store_middle(row, state)
        here = above

    @pl.when(at_first)
    def _():
        for f in range(3):
            middle[f, pl.ds(0, SUB), :] = middle[f, pl.ds(SUB, SUB), :]

    @pl.when(at_final)
    def _():
        for f in range(3):
            middle[f, pl.ds((band_rows + 1) * SUB, SUB), :] = middle[f, pl.ds(band_rows * SUB, SUB), :]

    edges2 = edge_fluxes[1]
    here = middle_row(0)
    flux = weighted(0, middle_row(-1), here)
    unroll2 = 8 if band_rows % 8 == 0 else 1

    def second_step(n, carry):
        here, flux = carry
        for i in range(unroll2):
            row = n * unroll2 + i
            above = middle_row(row + 1)
            state, flux = advance_row(row, here, above, flux, edges2)
            window = pl.ds(row, SUB, stride=band_rows)
            depth_out[window, :] = state[0]
            mom_out.at[0][window, :] = state[1]
            mom_out.at[1][window, :] = state[2]
            here = above
        return here, flux

    lax.fori_loop(0, band_rows // unroll2, second_step, (here, flux))


def dynamics(gravity, table, depth, mom, north, south, west, east, own_west, own_east):
    layers, band_rows = gravity.shape[0], depth.shape[0] // gravity.shape[0]
    block = SUB * band_rows
    smem = pl.BlockSpec(memory_space=pltpu.SMEM)
    whole = pl.BlockSpec(table.shape, lambda g: (0, 0))
    depth_spec = pl.BlockSpec((block, LANES), lambda g: (g, 0))
    mom_spec = pl.BlockSpec((2, block, LANES), lambda g: (0, g, 0))
    halo_spec = pl.BlockSpec((3, 2, SUB, LANES), lambda g: (0, 0, g, 0))
    return pl.pallas_call(
        functools.partial(dynamics_kernel, band_rows),
        grid=(layers // SUB,),
        out_shape=(
            jax.ShapeDtypeStruct(depth.shape, jnp.float32),
            jax.ShapeDtypeStruct(mom.shape, jnp.float32),
        ),
        in_specs=[smem, smem, whole, depth_spec, mom_spec] + [halo_spec] * 6,
        out_specs=(depth_spec, mom_spec),
        scratch_shapes=[pltpu.VMEM((3, (band_rows + 2) * SUB, LANES), jnp.float32)],
        compiler_params=params(),
        cost_estimate=pl.CostEstimate(
            flops=220 * depth.size, bytes_accessed=24 * depth.size, transcendentals=8 * depth.size
        ),
        name="dynamics",
    )(gravity, table, table, depth, mom, north, south, west, east, own_west, own_east)


def rows_kernel(depth_head, depth_tail, mom_head, mom_tail, head_out, tail_out):
    layers = depth_head.shape[0] // SUB
    fields = (
        (depth_head, depth_tail),
        (mom_head.at[0], mom_tail.at[0]),
        (mom_head.at[1], mom_tail.at[1]),
    )
    for f, (head, tail) in enumerate(fields):
        for which in range(2):
            head_out[f, which] = head[pl.ds(which, layers, stride=SUB), :]
            tail_out[f, which] = tail[pl.ds(SUB - 1 - which, layers, stride=SUB), :]


def edge_rows(layer_depth, momentum):
    layers, band_rows, _ = layer_depth.shape

    def kernel(depth_head, depth_tail, mom_head, mom_tail, head_out, tail_out):
        rows_kernel(
            depth_head.reshape(layers * SUB, LANES),
            depth_tail.reshape(layers * SUB, LANES),
            mom_head.reshape(2, layers * SUB, LANES),
            mom_tail.reshape(2, layers * SUB, LANES),
            head_out,
            tail_out,
        )

    final = band_rows // SUB - 1
    out = jax.ShapeDtypeStruct((3, 2, layers, LANES), jnp.float32)
    out_spec = pl.BlockSpec(out.shape, lambda i: (0, 0, 0, 0))
    return pl.pallas_call(
        kernel,
        grid=(1,),
        out_shape=(out, out),
        in_specs=[
            pl.BlockSpec((layers, SUB, LANES), lambda i: (0, 0, 0)),
            pl.BlockSpec((layers, SUB, LANES), lambda i: (0, final, 0)),
            pl.BlockSpec((2, layers, SUB, LANES), lambda i: (0, 0, 0, 0)),
            pl.BlockSpec((2, layers, SUB, LANES), lambda i: (0, 0, final, 0)),
        ],
        out_specs=(out_spec, out_spec),
        compiler_params=params(),
        cost_estimate=pl.CostEstimate(flops=0, bytes_accessed=1 << 20, transcendentals=0),
        name="edge_rows",
    )(layer_depth, layer_depth, momentum, momentum)


def columns_kernel(band_rows, depth_ref, mom_ref, north_ref, south_ref, west_out, east_out):
    lane = lane_index()
    for f, ref in enumerate((depth_ref, mom_ref.at[0], mom_ref.at[1])):
        parts = [jnp.ones((SUB, LANES), jnp.float32)] * 4
        for row in range(-1, band_rows + 1):
            if row < 0:
                x = north_ref[f, 0]
            elif row == band_rows:
                x = south_ref[f, 0]
            else:
                x = ref[pl.ds(row, SUB, stride=band_rows), :]
            if row >= 0:
                x = roll(x, row + 1)
            parts = [
                jnp.where(lane == (row + at) % LANES, x, part)
                for part, at in zip(parts, (1, 2, 0, LANES - 1))
            ]
        west_out[f, 0] = parts[0]
        west_out[f, 1] = roll(parts[1], LANES - 1)
        east_out[f, 0] = roll(parts[2], 1)
        east_out[f, 1] = roll(parts[3], 2)


def edge_columns(depth, mom, north, south, layers):
    band_rows = depth.shape[0] // layers
    block = SUB * band_rows
    halo_spec = pl.BlockSpec((3, 2, SUB, LANES), lambda g: (0, 0, g, 0))
    out = jax.ShapeDtypeStruct((3, 2, layers, LANES), jnp.float32)
    return pl.pallas_call(
        functools.partial(columns_kernel, band_rows),
        grid=(layers // SUB,),
        out_shape=(out, out),
        in_specs=[
            pl.BlockSpec((block, LANES), lambda g: (g, 0)),
            pl.BlockSpec((2, block, LANES), lambda g: (0, g, 0)),
            halo_spec,
            halo_spec,
        ],
        out_specs=(halo_spec, halo_spec),
        compiler_params=params(),
        cost_estimate=pl.CostEstimate(flops=12 * depth.size, bytes_accessed=12 * depth.size, transcendentals=0),
        name="edge_columns",
    )(depth, mom, north, south)


def shortwave_kernel(slots, fresh, absorb_ref, solar_ref, depth_ref, sun_ref, lit_ref, owner_ref, slot_ref, *rest):
    before_ref, heat_out, sent_out, scaled, total = rest[-5:]
    layers, rows, _ = depth_ref.shape
    bands = solar_ref.shape[1]
    sun = sun_ref[...]
    per_sun = -math.log2(math.e) / sun
    for k in range(layers):
        scaled[k] = depth_ref[k] * per_sun
    log_solar = jnp.log2(solar_ref[...])
    top = jnp.zeros((rows, LANES), jnp.float32)
    for first in range(0, bands, SUN_BANDS):
        chunk = range(first, min(first + SUN_BANDS, bands))
        paths = [jnp.broadcast_to(log_solar[:, b : b + 1], (rows, LANES)) for b in chunk]
        for path in paths:
            top = top + jnp.exp2(path)

        def layer(k, paths):
            depth = scaled[k]
            paths = [path + absorb_ref[b, k] * depth for path, b in zip(paths, chunk)]
            downs = [jnp.exp2(path) for path in paths]
            while len(downs) > 1:
                downs = [sum(downs[i : i + 2][1:], downs[i]) for i in range(0, len(downs), 2)]
            total[k] = downs[0] if first == 0 else total[k] + downs[0]
            return paths

        def layers_of(n, paths):
            for i in range(4):
                paths = layer(n * 4 + i, paths)
            return paths

        lax.fori_loop(0, layers // 4, layers_of, paths)
    lit = lit_ref[...] == 1
    lit_lanes = jnp.broadcast_to(lit_ref[...], (rows, LANES)) == 1
    above = top
    for k in range(layers):
        below = total[k]
        absorbed = sun * (above - below)
        heat_out[k] = jnp.where(lit_lanes, absorbed / depth_ref[k], 0.0)
        above = below
    mean = jnp.sum(sun * (top - above), axis=1, keepdims=True) * (1.0 / (layers * LANES))
    target = owner_ref[...] * slots + slot_ref[...]
    target = jnp.broadcast_to(jnp.where(lit, target, -1), (rows, LANES))
    placed = jnp.where(target == lane_index(rows), jnp.broadcast_to(mean, (rows, LANES)), 0.0)
    placed = jnp.sum(placed, axis=0, keepdims=True)

    @pl.when(pl.program_id(0) == 0)
    def _():
        sent_out[...] = placed if fresh else before_ref[...] + placed

    @pl.when(pl.program_id(0) > 0)
    def _():
        sent_out[...] += placed


def shortwave(slots, begin, end, absorption, solar, layer_depth, sun, lit, owner, slot, before, heating):
    layers, band_rows, _ = layer_depth.shape
    fresh = heating is None
    first = begin // SUN_ROWS
    cube = pl.BlockSpec((layers, SUN_ROWS, LANES), lambda i: (0, first + i, 0))
    flat = pl.BlockSpec((SUN_ROWS, LANES), lambda i: (first + i, 0))
    thin = pl.BlockSpec((SUN_ROWS, 1), lambda i: (first + i, 0))
    line = pl.BlockSpec((1, LANES), lambda i: (0, 0))
    operands = [absorption, solar, layer_depth, sun, lit, owner, slot]
    in_specs = [
        pl.BlockSpec(memory_space=pltpu.SMEM),
        pl.BlockSpec(solar.shape, lambda i: (0, 0)),
        cube,
        flat,
        thin,
        thin,
        thin,
    ]
    aliases = {}
    if not fresh:
        aliases = {len(operands): 0}
        operands.append(heating)
        in_specs.append(pl.BlockSpec(memory_space=pl.ANY))
    operands.append(before)
    in_specs.append(line)
    size = layers * (end - begin) * LANES * absorption.shape[0]
    return pl.pallas_call(
        functools.partial(shortwave_kernel, slots, fresh),
        grid=((end - begin) // SUN_ROWS,),
        out_shape=(
            jax.ShapeDtypeStruct(layer_depth.shape, jnp.float32),
            jax.ShapeDtypeStruct((1, LANES), jnp.float32),
        ),
        in_specs=in_specs,
        out_specs=(cube, line),
        scratch_shapes=[pltpu.VMEM((layers, SUN_ROWS, LANES), jnp.float32)] * 2,
        input_output_aliases=aliases,
        compiler_params=params(),
        cost_estimate=pl.CostEstimate(
            flops=4 * size, bytes_accessed=8 * size // absorption.shape[0], transcendentals=size
        ),
        name="shortwave",
    )(*operands)


def ledger_kernel(slots, counts_ref, table_ref, ledger_out):
    sources = table_ref.shape[0]
    here = lax.axis_index("lon")
    lane = lane_index()
    ledger = jnp.zeros((SUB, LANES), jnp.float32)
    start = jnp.int32(0)
    for s in range(sources):
        end = start + counts_ref[0, s]
        values = jnp.broadcast_to(table_ref[s : s + 1, :], (SUB, LANES))
        values = roll(values, lax.rem(start - here * slots + 2 * LANES, LANES))
        ledger = jnp.where((lane >= start) & (lane < end), values, ledger)
        start = end
    ledger_out[...] = ledger[:1, : ledger_out.shape[1]]


def ledger_of(slots, load, counts, table):
    return pl.pallas_call(
        functools.partial(ledger_kernel, slots),
        out_shape=jax.ShapeDtypeStruct((1, load), jnp.float32),
        in_specs=[pl.BlockSpec(memory_space=pltpu.SMEM), pl.BlockSpec(memory_space=pltpu.VMEM)],
        out_specs=pl.BlockSpec(memory_space=pltpu.VMEM),
        compiler_params=params(),
        name="ledger",
    )(counts, table)


def body(
    table,
    layer_depth,
    momentum,
    gravity,
    absorption,
    solar_flux,
    cos_zenith,
    sunlit,
    owner_index,
    slot_index,
    received_counts,
):
    layers, band_rows, width = layer_depth.shape
    lon_parts, lat_parts = lax.axis_size("lon"), lax.axis_size("lat")
    slots = band_rows // lon_parts
    depth = layer_depth.reshape(layers * band_rows, width)
    mom = momentum.reshape(2, layers * band_rows, width)
    solar = solar_flux.reshape(1, -1)

    head, tail = edge_rows(layer_depth, momentum)
    north = lax.ppermute(tail, "lat", [(i, i + 1) for i in range(lat_parts - 1)])
    south = lax.ppermute(head, "lat", [(i + 1, i) for i in range(lat_parts - 1)])

    half = band_rows // 2
    sun_args = (absorption, solar, layer_depth, cos_zenith, sunlit, owner_index, slot_index)
    heating, sent = shortwave(slots, 0, half, *sun_args, jnp.zeros((1, LANES), jnp.float32), None)

    own_west, own_east = edge_columns(depth, mom, north, south, layers)
    west = lax.ppermute(own_east, "lon", [(i, (i + 1) % lon_parts) for i in range(lon_parts)])
    east = lax.ppermute(own_west, "lon", [((i + 1) % lon_parts, i) for i in range(lon_parts)])

    heating, sent = shortwave(slots, half, band_rows, *sun_args, sent, heating)
    arrived = lax.all_gather(sent, "lon", axis=0, tiled=True)

    depth_new, mom_new = dynamics(
        gravity, table, depth, mom, north, south, west, east, own_west, own_east
    )
    ledger = ledger_of(slots, band_rows // 2, received_counts[0], arrived)
    return (
        depth_new.reshape(layer_depth.shape),
        mom_new.reshape(momentum.shape),
        heating,
        ledger[None],
    )


def solution(mesh):
    placed = (
        P(None, "lat", "lon"),
        P(None, None, "lat", "lon"),
        P(),
        P(),
        P(),
        P("lat", "lon"),
        P("lat", "lon"),
        P("lat", "lon"),
        P("lat", "lon"),
        P("lat", "lon", None),
    )

    def whole(layer_depth, *others):
        table = latitude_table(mesh.shape["lat"], layer_depth.shape[1] // mesh.shape["lat"])
        return jax.shard_map(
            functools.partial(body, table),
            mesh=mesh,
            in_specs=placed,
            out_specs=(
                P(None, "lat", "lon"),
                P(None, None, "lat", "lon"),
                P(None, "lat", "lon"),
                P("lat", "lon", None),
            ),
            check_vma=False,
        )(layer_depth, *others)

    return whole
```

```python
import functools
import math

import jax
import jax.numpy as jnp
import numpy as np
from jax import lax
from jax.experimental import pallas as pl
from jax.experimental.pallas import tpu as pltpu
from jax.sharding import PartitionSpec as P

COURANT = 0.06
CORIOLIS = 0.08
LAT_START = 0.35
LAT_SPAN = 0.62
LANES = 128
SUB = 8
SUN_ROWS = 32
SUN_BANDS = 7
SUN_LAYERS = 8
DEEP = 16
BLOCK_ROWS = 6
MIB = 1024 * 1024


def params(limit=24):
    return pltpu.CompilerParams(vmem_limit_bytes=limit * MIB)


def lane_index(rows=SUB):
    return lax.broadcasted_iota(jnp.int32, (rows, LANES), 1)


def latitude_table(lat_parts, band_rows):
    total = lat_parts * band_rows
    rows = np.arange(lat_parts)[:, None] * band_rows + np.arange(-2, LANES)[None, :]
    latitude = np.float32(LAT_START) + (rows.astype(np.float32) + np.float32(0.5)) * np.float32(LAT_SPAN / total)
    face = (np.float32(0.5) * (latitude[:, :-1] + latitude[:, 1:])).astype(np.float64)
    latitude = latitude.astype(np.float64)
    table = np.zeros((lat_parts, 8, LANES), np.float32)
    table[:, 0] = COURANT / np.cos(latitude[:, 1 : LANES + 1])
    table[:, 1] = np.cos(face[:, 1 : LANES + 1])
    table[:, 2] = np.cos(face[:, :LANES])
    table[:, 3] = CORIOLIS * np.sin(latitude[:, 1 : LANES + 1])
    return table.reshape(lat_parts * 8, LANES)


def cell(depth, east_mom, north_mom, gravity):
    inverse = 1.0 / depth
    east_vel = east_mom * inverse
    north_vel = north_mom * inverse
    weight = gravity * depth
    wave = weight * lax.rsqrt(weight)
    push = 0.5 * weight * depth
    cross = north_mom * east_vel
    return (
        depth,
        east_mom,
        north_mom,
        east_vel - wave,
        east_vel + wave,
        east_mom * east_vel + push,
        cross,
        north_vel - wave,
        north_vel + wave,
        north_mom * north_vel + push,
    )


def east_side(c):
    return (c[0], c[1], c[2], c[3], c[4], c[5], c[6])


def north_side(c):
    return (c[0], c[2], c[1], c[7], c[8], c[9], c[6])


def face(left, right):
    lower = jnp.minimum(jnp.minimum(left[3], right[3]), 0.0)
    upper = jnp.maximum(jnp.maximum(left[4], right[4]), 0.0)
    share = upper / (upper - lower)
    rise = right[1] - left[1]
    depth_flux = right[1] + share * (lower * (right[0] - left[0]) - rise)
    normal_flux = right[5] + share * (lower * rise - (right[5] - left[5]))
    other_flux = right[6] + share * (lower * (right[2] - left[2]) - (right[6] - left[6]))
    return depth_flux, normal_flux, other_flux


def turned(state, change, rate, turning):
    depth, east_mom, north_mom = (s - rate * c for s, c in zip(state, change))
    return depth, east_mom + turning * north_mom, north_mom - turning * east_mom


def roll(x, shift):
    return pltpu.roll(x, shift, 1)


def dynamics_kernel(
    band_rows,
    gravity_ref,
    table_ref,
    lanes_ref,
    depth_ref,
    mom_ref,
    north_ref,
    south_ref,
    west_ref,
    east_ref,
    own_west_ref,
    own_east_ref,
    depth_out,
    mom_out,
    first_state,
    middle_state,
    shifted,
    partial,
    east_fluxes,
    edge_fluxes,
):
    deep = depth_ref.shape[0] // band_rows
    group = pl.program_id(0)
    lat = lax.axis_index("lat")
    at_first = lat == 0
    at_final = lat == lax.axis_size("lat") - 1
    layer = lax.broadcasted_iota(jnp.int32, (deep, LANES), 0)
    gravity = jnp.zeros((deep, LANES), jnp.float32)
    for i in range(deep):
        gravity = jnp.where(layer == i, gravity_ref[group * deep + i], gravity)
    lane = lane_index(deep)
    is_first_lane = lane == 0
    is_last_lane = lane == LANES - 1

    both = jnp.concatenate([gravity, gravity], axis=0)
    lane2 = lane_index(2 * deep)
    low_edge = (lane2 == 0) & at_first
    high_edge = (lane2 == band_rows + 1) & at_final

    def column(west, east):
        fields = []
        for f in range(3):
            x = jnp.concatenate([west(f), east(f)], axis=0)
            x = jnp.where(low_edge, roll(x, LANES - 1), x)
            fields.append(jnp.where(high_edge, roll(x, 1), x))
        return cell(*fields, both)

    columns = [
        column(lambda f: west_ref[f, 1], lambda f: own_east_ref[f, 1]),
        column(lambda f: west_ref[f, 0], lambda f: own_east_ref[f, 0]),
        column(lambda f: own_west_ref[f, 0], lambda f: east_ref[f, 0]),
        column(lambda f: own_west_ref[f, 1], lambda f: east_ref[f, 1]),
    ]
    rate_of, upper_cos, lower_cos, turn_of = (
        jnp.broadcast_to(lanes_ref[pl.ds(lat * 8 + q, 1), :], (2 * deep, LANES)) for q in range(4)
    )
    fluxes = [face(east_side(a), east_side(b)) for a, b in zip(columns[:-1], columns[1:])]
    moved = []
    for k in (1, 2):
        c = columns[k]
        side = north_side(c)
        upper = face(side, tuple(roll(x, LANES - 1) for x in side))
        upper = (upper[0], upper[2], upper[1])
        change = tuple(
            fluxes[k][i] - fluxes[k - 1][i] + upper_cos * upper[i] - lower_cos * roll(upper[i], 1)
            for i in range(3)
        )
        moved.append(cell(*turned(c[:3], change, rate_of, turn_of), both))
    for step, edges in enumerate((fluxes[1], face(east_side(moved[0]), east_side(moved[1])))):
        for i in range(3):
            edge_fluxes[step, i] = edges[i]

    def at(index):
        start = index * deep
        return pl.ds(start if isinstance(start, int) else pl.multiple_of(start, SUB), deep)

    def store(ref, index, values):
        for f in range(3):
            ref[f, at(index), :] = values[f]

    def fetch(ref, index):
        return tuple(ref[f, at(index), :] for f in range(3))

    def inside(row):
        window = pl.ds(row, deep, stride=band_rows)
        return depth_ref[window, :], mom_ref.at[0][window, :], mom_ref.at[1][window, :]

    def outer(ref, which, clamped, edge_row):
        here = inside(edge_row)
        return tuple(jnp.where(clamped, here[f], ref[f, which]) for f in range(3))

    def rotate(row, raw):
        store(shifted, row + 1, tuple(roll(x, 1) for x in raw))

    def faces(state, offset, row, here, below):
        above = cell(*fetch(state, row + 1 + offset), gravity)
        upper = face(north_side(here), north_side(above))
        cos_upper = table_ref[lat * 8 + 1, row + 1]
        upper = (cos_upper * upper[0], cos_upper * upper[2], cos_upper * upper[1])
        rate = table_ref[lat * 8, row + 1]
        store(partial, row + 1, tuple(here[i] - rate * (upper[i] - below[i]) for i in range(3)))
        west = cell(*fetch(shifted, row + 1), gravity)
        store(east_fluxes, row + 1, face(east_side(west), east_side(here)))
        return above, upper

    def update(step, row):
        j = row + 1
        rate = table_ref[lat * 8, j]
        turning = table_ref[lat * 8 + 3, j]
        state = []
        for i in range(3):
            flux = east_fluxes[i, at(j), :]
            west_edge = roll(edge_fluxes[step, i, pl.ds(0, deep), :], lax.rem(2 * LANES - j, LANES))
            east_edge = roll(edge_fluxes[step, i, pl.ds(deep, deep), :], lax.rem(2 * LANES - 1 - j, LANES))
            west_flux = jnp.where(is_first_lane, west_edge, flux)
            east_flux = jnp.where(is_last_lane, east_edge, roll(flux, LANES - 1))
            state.append(partial[i, at(j), :] - rate * (east_flux - west_flux))
        depth, east_mom, north_mom = state
        return depth, east_mom + turning * north_mom, north_mom - turning * east_mom

    def start(state, offset, row):
        below = cell(*fetch(state, row - 1 + offset), gravity)
        here = cell(*fetch(state, row + offset), gravity)
        flux = face(north_side(below), north_side(here))
        cos_lower = table_ref[lat * 8 + 2, row + 1]
        return here, (cos_lower * flux[0], cos_lower * flux[2], cos_lower * flux[1])

    def walk(first_row, rows, prepare, middle, finish):
        blocks, left = divmod(rows, BLOCK_ROWS)

        def span(n):
            return [first_row + n * BLOCK_ROWS + i for i in range(BLOCK_ROWS)]

        def each(f, n):
            for row in span(n):
                f(row)

        def middle_rows(rows_of, carry):
            for row in rows_of:
                carry = middle(row, carry)
            return carry

        each(prepare, 0)
        each(prepare, 1)
        carry = middle_rows(span(0), None)

        def full(n, carry):
            each(finish, n - 1)
            carry = middle_rows(span(n), carry)
            each(prepare, n + 1)
            return carry

        carry = lax.fori_loop(1, blocks - 1, full, carry)
        tail = [first_row + blocks * BLOCK_ROWS + i for i in range(left)]
        each(finish, blocks - 2)
        carry = middle_rows(span(blocks - 1), carry)
        for row in tail:
            prepare(row)
        each(finish, blocks - 1)
        middle_rows(tail, carry)
        for row in tail:
            finish(row)

    for row, ref, which, clamped, edge_row in (
        (-2, north_ref, 1, at_first, 0),
        (-1, north_ref, 0, at_first, 0),
        (band_rows, south_ref, 0, at_final, band_rows - 1),
        (band_rows + 1, south_ref, 1, at_final, band_rows - 1),
    ):
        raw = outer(ref, which, clamped, edge_row)
        store(first_state, row + 2, raw)
        if -1 <= row <= band_rows:
            rotate(row, raw)

    def prepare1(row):
        ahead = jnp.minimum(row + 1, band_rows - 1)
        raw = inside(ahead)
        store(first_state, ahead + 2, raw)
        rotate(ahead, raw)

    def middle1(row, carry):
        if carry is None:
            carry = start(first_state, 2, row)
        return faces(first_state, 2, row, *carry)

    def finish1(row):
        store(middle_state, row + 1, update(0, row))

    walk(-1, band_rows + 2, prepare1, middle1, finish1)

    @pl.when(at_first)
    def _():
        store(middle_state, 0, fetch(middle_state, 1))

    @pl.when(at_final)
    def _():
        store(middle_state, band_rows + 1, fetch(middle_state, band_rows))

    def prepare2(row):
        rotate(row, fetch(middle_state, row + 1))

    def middle2(row, carry):
        if carry is None:
            carry = start(middle_state, 1, row)
        return faces(middle_state, 1, row, *carry)

    def finish2(row):
        window = pl.ds(row, deep, stride=band_rows)
        state = update(1, row)
        depth_out[window, :] = state[0]
        mom_out.at[0][window, :] = state[1]
        mom_out.at[1][window, :] = state[2]

    walk(0, band_rows, prepare2, middle2, finish2)


def dynamics(gravity, table, depth, mom, north, south, west, east, own_west, own_east):
    layers, band_rows = gravity.shape[0], depth.shape[0] // gravity.shape[0]
    deep = DEEP
    block = deep * band_rows
    smem = pl.BlockSpec(memory_space=pltpu.SMEM)
    whole = pl.BlockSpec(table.shape, lambda g: (0, 0))
    depth_spec = pl.BlockSpec((block, LANES), lambda g: (g, 0))
    mom_spec = pl.BlockSpec((2, block, LANES), lambda g: (0, g, 0))
    halo_spec = pl.BlockSpec((3, 2, deep, LANES), lambda g: (0, 0, g, 0))
    rows_of = lambda rows: pltpu.VMEM((3, rows * deep, LANES), jnp.float32)
    return pl.pallas_call(
        functools.partial(dynamics_kernel, band_rows),
        grid=(layers // deep,),
        out_shape=(
            jax.ShapeDtypeStruct(depth.shape, jnp.float32),
            jax.ShapeDtypeStruct(mom.shape, jnp.float32),
        ),
        in_specs=[smem, smem, whole, depth_spec, mom_spec] + [halo_spec] * 6,
        out_specs=(depth_spec, mom_spec),
        scratch_shapes=[rows_of(band_rows + 4)]
        + [rows_of(band_rows + 2)] * 4
        + [pltpu.VMEM((2, 3, 2 * deep, LANES), jnp.float32)],
        compiler_params=params(),
        cost_estimate=pl.CostEstimate(
            flops=220 * depth.size, bytes_accessed=24 * depth.size, transcendentals=8 * depth.size
        ),
        name="dynamics",
    )(gravity, table, table, depth, mom, north, south, west, east, own_west, own_east)


def rows_kernel(depth_head, depth_tail, mom_head, mom_tail, head_out, tail_out):
    layers = depth_head.shape[0] // SUB
    fields = (
        (depth_head, depth_tail),
        (mom_head.at[0], mom_tail.at[0]),
        (mom_head.at[1], mom_tail.at[1]),
    )
    for f, (head, tail) in enumerate(fields):
        for which in range(2):
            head_out[f, which] = head[pl.ds(which, layers, stride=SUB), :]
            tail_out[f, which] = tail[pl.ds(SUB - 1 - which, layers, stride=SUB), :]


def edge_rows(layer_depth, momentum):
    layers, band_rows, _ = layer_depth.shape

    def kernel(depth_head, depth_tail, mom_head, mom_tail, head_out, tail_out):
        rows_kernel(
            depth_head.reshape(layers * SUB, LANES),
            depth_tail.reshape(layers * SUB, LANES),
            mom_head.reshape(2, layers * SUB, LANES),
            mom_tail.reshape(2, layers * SUB, LANES),
            head_out,
            tail_out,
        )

    final = band_rows // SUB - 1
    out = jax.ShapeDtypeStruct((3, 2, layers, LANES), jnp.float32)
    out_spec = pl.BlockSpec(out.shape, lambda i: (0, 0, 0, 0))
    return pl.pallas_call(
        kernel,
        grid=(1,),
        out_shape=(out, out),
        in_specs=[
            pl.BlockSpec((layers, SUB, LANES), lambda i: (0, 0, 0)),
            pl.BlockSpec((layers, SUB, LANES), lambda i: (0, final, 0)),
            pl.BlockSpec((2, layers, SUB, LANES), lambda i: (0, 0, 0, 0)),
            pl.BlockSpec((2, layers, SUB, LANES), lambda i: (0, 0, final, 0)),
        ],
        out_specs=(out_spec, out_spec),
        compiler_params=params(60),
        cost_estimate=pl.CostEstimate(flops=0, bytes_accessed=1 << 20, transcendentals=0),
        name="edge_rows",
    )(layer_depth, layer_depth, momentum, momentum)


def columns_kernel(band_rows, depth_ref, mom_ref, north_ref, south_ref, west_out, east_out):
    lane = lane_index()
    for f, ref in enumerate((depth_ref, mom_ref.at[0], mom_ref.at[1])):
        parts = [jnp.ones((SUB, LANES), jnp.float32)] * 4
        for row in range(-1, band_rows + 1):
            if row < 0:
                x = north_ref[f, 0]
            elif row == band_rows:
                x = south_ref[f, 0]
            else:
                x = ref[pl.ds(row, SUB, stride=band_rows), :]
            if row >= 0:
                x = roll(x, row + 1)
            parts = [
                jnp.where(lane == (row + at) % LANES, x, part)
                for part, at in zip(parts, (1, 2, 0, LANES - 1))
            ]
        west_out[f, 0] = parts[0]
        west_out[f, 1] = roll(parts[1], LANES - 1)
        east_out[f, 0] = roll(parts[2], 1)
        east_out[f, 1] = roll(parts[3], 2)


def edge_columns(depth, mom, north, south, layers):
    band_rows = depth.shape[0] // layers
    block = SUB * band_rows
    halo_spec = pl.BlockSpec((3, 2, SUB, LANES), lambda g: (0, 0, g, 0))
    out = jax.ShapeDtypeStruct((3, 2, layers, LANES), jnp.float32)
    return pl.pallas_call(
        functools.partial(columns_kernel, band_rows),
        grid=(layers // SUB,),
        out_shape=(out, out),
        in_specs=[
            pl.BlockSpec((block, LANES), lambda g: (g, 0)),
            pl.BlockSpec((2, block, LANES), lambda g: (0, g, 0)),
            halo_spec,
            halo_spec,
        ],
        out_specs=(halo_spec, halo_spec),
        compiler_params=params(),
        cost_estimate=pl.CostEstimate(flops=12 * depth.size, bytes_accessed=12 * depth.size, transcendentals=0),
        name="edge_columns",
    )(depth, mom, north, south)


def shortwave_kernel(slots, first, fresh, absorb_ref, solar_ref, depth_ref, sun_ref, lit_ref, owner_ref, slot_ref, *rest):
    heat_out, sent_out, scaled, total = rest[-4:]
    layers, rows, _ = depth_ref.shape
    bands = solar_ref.shape[1]
    sun = sun_ref[...]
    per_sun = -math.log2(math.e) / sun
    for k in range(layers):
        scaled[k] = depth_ref[k] * per_sun
    log_solar = jnp.log2(solar_ref[...])
    top = jnp.zeros((rows, LANES), jnp.float32)
    for begin in range(0, bands, SUN_BANDS):
        chunk = range(begin, min(begin + SUN_BANDS, bands))
        paths = [jnp.broadcast_to(log_solar[:, b : b + 1], (rows, LANES)) for b in chunk]
        for path in paths:
            top = top + jnp.exp2(path)

        def layer(k, paths):
            depth = scaled[k]
            paths = [path + absorb_ref[k, b] * depth for path, b in zip(paths, chunk)]
            downs = [None, None]
            for i, path in enumerate(paths):
                down = jnp.exp2(path)
                downs[i % 2] = down if downs[i % 2] is None else downs[i % 2] + down
            downs = [sum(downs[1:], downs[0])]
            total[k] = downs[0] if begin == 0 else total[k] + downs[0]
            return paths

        def layers_of(n, paths):
            for i in range(SUN_LAYERS):
                paths = layer(n * SUN_LAYERS + i, paths)
            return paths

        lax.fori_loop(0, layers // SUN_LAYERS, layers_of, paths)
    place = jnp.where(lit_ref[...] == 1, owner_ref[...] * slots + slot_ref[...], -1).astype(jnp.float32)
    band_rows = place.shape[1]
    row = (first + pl.program_id(0)) * rows + lax.broadcasted_iota(jnp.int32, (rows, band_rows), 0)
    own = row == lax.broadcasted_iota(jnp.int32, (rows, band_rows), 1)
    place = jnp.sum(jnp.where(own, jnp.broadcast_to(place, own.shape), 0.0), axis=1, keepdims=True)
    place = jnp.broadcast_to(place, (rows, LANES))
    lit_lanes = place >= 0.0
    above = top
    for k in range(layers):
        below = total[k]
        absorbed = sun * (above - below)
        heat_out[k] = jnp.where(lit_lanes, absorbed / depth_ref[k], 0.0)
        above = below
    mean = jnp.sum(sun * (top - above), axis=1, keepdims=True) * (1.0 / (layers * LANES))
    placed = jnp.where(
        place == lane_index(rows).astype(jnp.float32), jnp.broadcast_to(mean, (rows, LANES)), 0.0
    )
    placed = jnp.broadcast_to(jnp.sum(placed, axis=0, keepdims=True), sent_out.shape)

    @pl.when(pl.program_id(0) == 0)
    def _():
        sent_out[...] = placed if fresh else rest[1][...] + placed

    @pl.when(pl.program_id(0) > 0)
    def _():
        sent_out[...] += placed


def shortwave(slots, begin, end, absorption, solar, layer_depth, sun, lit, owner, slot, before, heating):
    layers, band_rows, _ = layer_depth.shape
    fresh = heating is None
    first = begin // SUN_ROWS
    cube = pl.BlockSpec((layers, SUN_ROWS, LANES), lambda i: (0, first + i, 0))
    flat = pl.BlockSpec((SUN_ROWS, LANES), lambda i: (first + i, 0))
    thin = pl.BlockSpec((1, band_rows), lambda i: (0, 0))
    parts = band_rows // slots
    line = pl.BlockSpec((parts, LANES), lambda i: (0, 0))
    operands = [absorption, solar, layer_depth, sun, lit, owner, slot]
    in_specs = [
        pl.BlockSpec(memory_space=pltpu.SMEM),
        pl.BlockSpec(solar.shape, lambda i: (0, 0)),
        cube,
        flat,
        thin,
        thin,
        thin,
    ]
    aliases = {}
    if not fresh:
        aliases = {len(operands): 0}
        operands.append(heating)
        in_specs.append(pl.BlockSpec(memory_space=pl.ANY))
        operands.append(before)
        in_specs.append(line)
    size = layers * (end - begin) * LANES * absorption.shape[1]
    return pl.pallas_call(
        functools.partial(shortwave_kernel, slots, first, fresh),
        grid=((end - begin) // SUN_ROWS,),
        out_shape=(
            jax.ShapeDtypeStruct(layer_depth.shape, jnp.float32),
            jax.ShapeDtypeStruct((parts, LANES), jnp.float32),
        ),
        in_specs=in_specs,
        out_specs=(cube, line),
        scratch_shapes=[pltpu.VMEM((layers, SUN_ROWS, LANES), jnp.float32)] * 2,
        input_output_aliases=aliases,
        compiler_params=params(),
        cost_estimate=pl.CostEstimate(
            flops=4 * size, bytes_accessed=8 * size // absorption.shape[1], transcendentals=size
        ),
        name="shortwave",
    )(*operands)


def ledger_kernel(slots, counts_ref, table_ref, ledger_out):
    sources = table_ref.shape[0]
    here = lax.axis_index("lon")
    lane = lane_index()
    ledger = jnp.zeros((SUB, LANES), jnp.float32)
    start = jnp.int32(0)
    for s in range(sources):
        end = start + counts_ref[0, s]
        values = jnp.broadcast_to(table_ref[s : s + 1, :], (SUB, LANES))
        values = roll(values, lax.rem(start - here * slots + 2 * LANES, LANES))
        ledger = jnp.where((lane >= start) & (lane < end), values, ledger)
        start = end
    ledger_out[...] = ledger[:1, : ledger_out.shape[1]]


def ledger_of(slots, load, counts, table):
    return pl.pallas_call(
        functools.partial(ledger_kernel, slots),
        out_shape=jax.ShapeDtypeStruct((1, load), jnp.float32),
        in_specs=[pl.BlockSpec(memory_space=pltpu.SMEM), pl.BlockSpec(memory_space=pltpu.VMEM)],
        out_specs=pl.BlockSpec(memory_space=pltpu.VMEM),
        compiler_params=params(),
        name="ledger",
    )(counts, table)


def body(
    table,
    layer_depth,
    momentum,
    gravity,
    absorption,
    solar_flux,
    cos_zenith,
    sunlit,
    owner_index,
    slot_index,
    received_counts,
):
    layers, band_rows, width = layer_depth.shape
    lon_parts, lat_parts = lax.axis_size("lon"), lax.axis_size("lat")
    slots = band_rows // lon_parts
    depth = layer_depth.reshape(layers * band_rows, width)
    mom = momentum.reshape(2, layers * band_rows, width)
    solar = solar_flux.reshape(1, -1)

    head, tail = edge_rows(layer_depth, momentum)
    north = lax.ppermute(tail, "lat", [(i, i + 1) for i in range(lat_parts - 1)])
    south = lax.ppermute(head, "lat", [(i + 1, i) for i in range(lat_parts - 1)])

    half = band_rows // 2
    by_row = (x.reshape(1, band_rows) for x in (sunlit, owner_index, slot_index))
    sun_args = (absorption.T, solar, layer_depth, cos_zenith, *by_row)
    heating, sent = shortwave(slots, 0, half, *sun_args, None, None)
    north, south, sent = lax.optimization_barrier((north, south, sent))

    own_west, own_east = edge_columns(depth, mom, north, south, layers)
    west = lax.ppermute(own_east, "lon", [(i, (i + 1) % lon_parts) for i in range(lon_parts)])
    east = lax.ppermute(own_west, "lon", [((i + 1) % lon_parts, i) for i in range(lon_parts)])

    heating, sent = shortwave(slots, half, band_rows, *sun_args, sent, heating)
    arrived = lax.all_to_all(sent, "lon", split_axis=0, concat_axis=0, tiled=True)
    west, east, sent = lax.optimization_barrier((west, east, sent))

    depth_new, mom_new = dynamics(
        gravity, table, depth, mom, north, south, west, east, own_west, own_east
    )
    arrived, depth_new = lax.optimization_barrier((arrived, depth_new))
    ledger = ledger_of(slots, band_rows // 2, received_counts[0], arrived)
    return (
        depth_new.reshape(layer_depth.shape),
        mom_new.reshape(momentum.shape),
        heating,
        ledger[None],
    )


def solution(mesh):
    placed = (
        P(None, "lat", "lon"),
        P(None, None, "lat", "lon"),
        P(),
        P(),
        P(),
        P("lat", "lon"),
        P("lat", "lon"),
        P("lat", "lon"),
        P("lat", "lon"),
        P("lat", "lon", None),
    )

    def whole(layer_depth, *others):
        table = latitude_table(mesh.shape["lat"], layer_depth.shape[1] // mesh.shape["lat"])
        return jax.shard_map(
            functools.partial(body, table),
            mesh=mesh,
            in_specs=placed,
            out_specs=(
                P(None, "lat", "lon"),
                P(None, None, "lat", "lon"),
                P(None, "lat", "lon"),
                P("lat", "lon", None),
            ),
            check_vma=False,
        )(layer_depth, *others)

    return whole
```
